32 devices in a mesh: dp: 2 (over x), row: 4 (over z), col: 4 (over y, core).
Axes of the slice: x: 2, y: 2, z: 4, core: 2. Of those that a mesh axis runs over, the one named last changes fastest.
Arguments:
- inputs: bfloat16 [4096, 2048], P('dp', ('row', 'col')), may hold values from -32 to 32
- segment_ids: int32 [2, 2048], P('dp'), may hold values from 0 to 7, never falling along the last dimension, each value on 1 to 1024 neighbouring positions
- attn_gain: bfloat16 [2048], P(('row', 'col')), may hold values from 0.25 to 1.75
- attn_shift: bfloat16 [2048], P(('row', 'col')), may hold values from -4 to 4
- query_weight: bfloat16 [2048, 2048], P('row', 'col'), may hold values from -0.1875 to 0.1875
- query_bias: bfloat16 [2048], P('col'), may hold values from -4 to 4
- key_weight: bfloat16 [2048, 2048], P('row', 'col'), may hold values from -0.1875 to 0.1875
- value_weight: bfloat16 [2048, 2048], P('row', 'col'), may hold values from -0.125 to 0.125
- value_bias: bfloat16 [2048], P('col'), may hold values from -6 to 6
- output_weight: bfloat16 [2048, 2048], P('col', 'row'), may hold values from -0.375 to 0.375
- output_bias: bfloat16 [2048], P(('row', 'col')), may hold values from -4 to 4
- mlp_gain: bfloat16 [2048], P(('row', 'col')), may hold values from 0.25 to 1.75
- mlp_shift: bfloat16 [2048], P(('row', 'col')), may hold values from -4 to 4
- up_weight: bfloat16 [2048, 8192], P('row', 'col'), may hold values from -0.125 to 0.125
- up_bias: bfloat16 [8192], P('col'), may hold values from -6 to 6
- down_weight: bfloat16 [8192, 2048], P('col', 'row'), may hold values from -0.0625 to 0.0625
- down_bias: bfloat16 [2048], P(('row', 'col')), may hold values from -4 to 4
- cotangent: bfloat16 [4096, 2048], P('dp', ('row', 'col')), may hold values from -6 to 6
Outputs:
- result: bfloat16 [4096, 2048], P('dp', ('row', 'col'))
- input_grad: float32 [4096, 2048], P('dp', ('row', 'col'))
- attn_gain_grad: float32 [2048], P(('row', 'col'))
- attn_shift_grad: float32 [2048], P(('row', 'col'))
- query_weight_grad: float32 [2048, 2048], P('row', 'col')
- query_bias_grad: float32 [2048], P('col')
- key_weight_grad: float32 [2048, 2048], P('row', 'col')
- value_weight_grad: float32 [2048, 2048], P('row', 'col')
- value_bias_grad: float32 [2048], P('col')
- output_weight_grad: float32 [2048, 2048], P('col', 'row')
- output_bias_grad: float32 [2048], P(('row', 'col'))
- mlp_gain_grad: float32 [2048], P(('row', 'col'))
- mlp_shift_grad: float32 [2048], P(('row', 'col'))
- up_weight_grad: float32 [2048, 8192], P('row', 'col')
- up_bias_grad: float32 [8192], P('col')
- down_weight_grad: float32 [8192, 2048], P('col', 'row')
- down_bias_grad: float32 [2048], P(('row', 'col'))
The draws below stay inside these ranges and needn't reach their ends.
Inputs may be any that keep to these rules, and one draw needn't show every extreme that they name: `segment_ids`: document numbers never fall along a sequence; a document holds 1 to 1024 tokens, and one holds exactly that many.
All inputs are finite; a program needn't handle non-finite values.
Results may differ from the reference program's by a relative error of at most 0.012.
The reference program's roundings to bfloat16 on the way count: a program that leaves them out, or rounds other values in their place, can miss the bound.
Values may be sent and summed in bfloat16 or wider, within the bound.
No kernel may reach another device: no remote copies, remote signals or barrier semaphores. Data moves between devices by JAX's collectives and lax.ppermute only.
A program may use at most 192 MiB of HBM per device.

```python
import math
import jax
import jax.numpy as jnp
import numpy as np
from jax import lax

D = 2048
H = 16
HD = 128
FF = 8192
TOK_DEV = 2048
DOCS = 8
SEQS = 2
TOKENS = 4096


def draw_inputs(key, part):
    key_entries, key_columns, key_tokens = jax.random.split(key, 3)
    column_pos = jnp.arange(D, dtype=jnp.float32) / D
    column_scale = 0.6 * jnp.power(3.0, column_pos) * jnp.exp(jax.random.uniform(key_columns, (D,), jnp.float32, -0.35, 0.35))
    token_scale = jnp.exp(jax.random.uniform(key_tokens, (TOKENS, 1), jnp.float32, -0.7, 0.7))
    entries = jnp.clip(jax.random.normal(key_entries, (TOKENS, D), jnp.float32), -6.0, 6.0)
    return (entries * column_scale * token_scale).astype(jnp.bfloat16)


def block_scale(stream_key, shape, pieces, low, top_value):
    loudness, own = 1.0, jax.random.fold_in(stream_key, 6)
    for position, parts in pieces:
        steps = jnp.exp(jax.random.uniform(jax.random.fold_in(own, position), (parts,), jnp.float32, low / len(pieces), top_value / len(pieces)))
        loudness = loudness * jnp.repeat(steps, shape[position] // parts).reshape([-1 if axis == position else 1 for axis in range(len(shape))])
    return loudness


def profile(number_of, total, reach, slope):
    weights = [(1 << 20) // math.isqrt(grade ** slope) + 1 for grade in range(2, number_of + 1)]
    rest, given = total - reach - (number_of - 1), [1] * (number_of - 1)
    while rest > 0:
        candidates = [i for i in range(number_of - 1) if given[i] < reach]
        whole, left = sum([weights[i] for i in candidates]), rest
        for i in candidates:
            more = min(reach - given[i], max(1, left * weights[i] // whole), rest)
            given[i] = given[i] + more
            rest = rest - more
    return np.array([reach] + given)


def ragged_sizes(rng, number_of, total, reach, slope):
    if number_of == 2:
        one = jax.random.randint(rng, (), max(1, total - reach), min(reach, total - 1) + 1)
        return jnp.stack([one, total - one])
    sizes = jnp.asarray(profile(number_of, total, reach, slope), jnp.int32)
    couples = (number_of - 1) // 2
    giver, receiver = sizes[1:1 + 2 * couples:2], sizes[2:2 + 2 * couples:2]
    margin = jnp.minimum(giver - 1, reach - receiver)
    shifted = jax.random.randint(jax.random.fold_in(rng, 1), (couples,), 0, 1 << 20) % (margin + 1)
    sizes = sizes.at[1:1 + 2 * couples:2].set(giver - shifted).at[2:2 + 2 * couples:2].set(receiver + shifted)
    return sizes[jax.random.permutation(jax.random.fold_in(rng, 2), number_of)]


def scatter_about(rng, extent, width, bound, cuts=(), kind=jnp.bfloat16):
    values = width * jax.random.normal(rng, extent, jnp.float32)
    if cuts:
        values = values * block_scale(rng, extent, cuts, -0.22, 0.18)
    return jnp.clip(values, -bound, bound).astype(kind)


def setup_inputs(seed: int = 0) -> dict:
    key_list = jax.random.split(jax.random.key(seed), 19)
    inputs = draw_inputs(jax.random.fold_in(key_list[18], 71), 0)
    segment_ids = jax.vmap(lambda own: jnp.searchsorted(jnp.cumsum(ragged_sizes(own, DOCS, TOK_DEV, TOK_DEV // 2, 2)), jnp.arange(TOK_DEV), side="right"))(jax.random.split(key_list[1], SEQS)).reshape((SEQS, TOK_DEV)).astype(jnp.int32)
    attn_gain = jnp.clip(1.0 + 0.15 * jax.random.normal(key_list[2], (D,), jnp.float32), 0.25, 1.75).astype(jnp.bfloat16)
    attn_shift = scatter_about(key_list[3], (D,), 0.3, 4.0, ((0, 16),))
    query_weight = scatter_about(key_list[4], (D, D), (D // 2) ** -0.5, 0.1875, ((0, 4), (1, 4)))
    query_bias = scatter_about(key_list[5], (D,), 0.3, 4.0, ((0, 4),))
    key_weight = scatter_about(key_list[6], (D, D), (D // 2) ** -0.5, 0.1875, ((0, 4), (1, 4)))
    value_weight = scatter_about(key_list[7], (D, D), D ** -0.5, 0.125, ((0, 4), (1, 4)))
    value_bias = scatter_about(key_list[8], (D,), 0.5, 6.0, ((0, 4),))
    output_weight = scatter_about(key_list[9], (D, D), (D // 8) ** -0.5, 0.375, ((0, 4), (1, 4)))
    output_bias = scatter_about(key_list[10], (D,), 0.3, 4.0, ((0, 16),))
    mlp_gain = jnp.clip(1.0 + 0.15 * jax.random.normal(key_list[11], (D,), jnp.float32), 0.25, 1.75).astype(jnp.bfloat16)
    mlp_shift = scatter_about(key_list[12], (D,), 0.3, 4.0, ((0, 16),))
    up_weight = scatter_about(key_list[13], (D, FF), D ** -0.5, 0.125, ((0, 4), (1, 4)))
    up_bias = scatter_about(key_list[14], (FF,), 0.5, 6.0, ((0, 4),))
    down_weight = scatter_about(key_list[15], (FF, D), FF ** -0.5, 0.0625, ((0, 4), (1, 4)))
    down_bias = scatter_about(key_list[16], (D,), 0.3, 4.0, ((0, 16),))
    cotangent = scatter_about(key_list[17], (TOKENS, D), 1.0, 6.0, ((0, 2), (1, 16)))
    return dict(inputs=inputs, segment_ids=segment_ids, attn_gain=attn_gain, attn_shift=attn_shift, query_weight=query_weight, query_bias=query_bias, key_weight=key_weight, value_weight=value_weight, value_bias=value_bias, output_weight=output_weight, output_bias=output_bias, mlp_gain=mlp_gain, mlp_shift=mlp_shift, up_weight=up_weight, up_bias=up_bias, down_weight=down_weight, down_bias=down_bias, cotangent=cotangent)


@jax.custom_vjp
def low(v):
    return lax.optimization_barrier(v.astype(jnp.bfloat16)).astype(jnp.float32)

@jax.custom_vjp
def low_back(v):
    return v

def low_keep(v):
    return (low(v), None)

def low_pass(kept, grad):
    return (grad,)

def back_keep(v):
    return (v, None)

def back_low(kept, grad):
    return (low(grad),)
low.defvjp(low_keep, low_pass)
low_back.defvjp(back_keep, back_low)
epsilon = 1e-05
negative_fill = -1000000000.0

def matmul(left, right):
    return jnp.dot(left, right, precision=lax.Precision.HIGHEST)

def layer_norm(values, gain_values, shift_values):
    center = lax.optimization_barrier(jnp.mean(values, axis=-1, keepdims=True))
    spread = lax.optimization_barrier(jnp.mean(jnp.square(values - center), axis=-1, keepdims=True))
    return (values - center) * lax.rsqrt(spread + epsilon) * gain_values + shift_values

def attention(queries, key_rows, value_rows, segment_ids):
    sequences = segment_ids.shape[0]
    length = segment_ids.shape[1]
    block_len = min(512, length)
    blocks = length // block_len
    scaling = 1.0 / jnp.sqrt(jnp.float32(HD))
    positions = jnp.arange(length, dtype=jnp.int32)
    query_all = queries.reshape(sequences, length, H, HD)
    key_all = key_rows.reshape(sequences, length, H, HD)
    value_all = value_rows.reshape(sequences, length, H, HD)

    def one_sequence(packed):
        seq_query, seq_key, seq_value, seq_segment = packed

        @jax.checkpoint
        def one_block(block_index):
            offset = block_index * block_len
            query_blk = lax.dynamic_slice_in_dim(seq_query, offset, block_len, 0)
            own_segment = lax.dynamic_slice_in_dim(seq_segment, offset, block_len, 0)
            own_position = offset + jnp.arange(block_len, dtype=jnp.int32)
            allowed = (own_segment[:, None] == seq_segment[None, :]) & (own_position[:, None] >= positions[None, :])
            scores = jnp.einsum('qhd,khd->hqk', query_blk, seq_key, precision=lax.Precision.HIGHEST)
            scores = low_back(scaling * scores)
            masked = jnp.where(allowed[None, :, :], scores, negative_fill)
            top_score = lax.optimization_barrier(jnp.max(masked, axis=-1, keepdims=True))
            exponent_terms = jnp.exp(masked - top_score)
            softmax_rows = low(exponent_terms / lax.optimization_barrier(jnp.sum(exponent_terms, axis=-1, keepdims=True)))
            return jnp.einsum('hqk,khd->qhd', softmax_rows, seq_value, precision=lax.Precision.HIGHEST)
        outcome = lax.map(one_block, jnp.arange(blocks, dtype=jnp.int32))
        return outcome.reshape(length, H * HD)
    attended = lax.map(one_sequence, (query_all, key_all, value_all, segment_ids))
    return attended.reshape(sequences * length, H * HD)

def forward(inputs, attn_gain, attn_shift, query_weight, query_bias, key_weight, value_weight, value_bias, output_weight, output_bias, mlp_gain, mlp_shift, up_weight, up_bias, down_weight, down_bias, segment_ids):
    first_norm = low(layer_norm(inputs, attn_gain, attn_shift))
    queries = low(low_back(matmul(first_norm, query_weight) + query_bias))
    key_rows = low(low_back(matmul(first_norm, key_weight)))
    value_rows = low(low_back(matmul(first_norm, value_weight) + value_bias))
    attended = low(low_back(attention(queries, key_rows, value_rows, segment_ids)))
    after_attn = inputs + low_back(matmul(attended, output_weight)) + output_bias
    second_norm = low(layer_norm(after_attn, mlp_gain, mlp_shift))
    pre_act = low_back(matmul(second_norm, up_weight) + up_bias)
    hidden = low(jax.nn.gelu(pre_act, approximate=False))
    return after_attn + low_back(matmul(hidden, down_weight)) + down_bias

def reference(inputs, segment_ids, attn_gain, attn_shift, query_weight, query_bias, key_weight, value_weight, value_bias, output_weight, output_bias, mlp_gain, mlp_shift, up_weight, up_bias, down_weight, down_bias, cotangent):
    params = (inputs, attn_gain, attn_shift, query_weight, query_bias, key_weight, value_weight, value_bias, output_weight, output_bias, mlp_gain, mlp_shift, up_weight, up_bias, down_weight, down_bias)
    floats = tuple((array_one.astype(jnp.float32) for array_one in params))

    def whole_layer(*floats_in):
        return forward(*floats_in, segment_ids)
    result, pullback = jax.vjp(whole_layer, *floats)
    gradients = pullback(cotangent.astype(jnp.float32))
    return (result.astype(jnp.bfloat16), gradients[0], gradients[1], gradients[2], gradients[3], gradients[4], gradients[5], gradients[6], gradients[7], gradients[8], gradients[9], gradients[10], gradients[11], gradients[12], gradients[13], gradients[14], gradients[15])
```

```python
import math

import jax
import jax.numpy as jnp
from jax import lax
from jax.sharding import PartitionSpec as P

HD = 128
epsilon = 1e-05
negative_fill = -1000000000.0
root_half = 0.7071067811865476
inverse_root_tau = 0.3989422804014327
BF = jnp.bfloat16
F32 = jnp.float32


def contract(left, right, left_dim, right_dim):
    return lax.dot_general(
        left, right, (((left_dim,), (right_dim,)), ((), ())), preferred_element_type=F32
    )


def after(values, anchor):
    return lax.optimization_barrier((values, anchor))[0]


def swap(values, k):
    size = lax.axis_size("col")
    return lax.ppermute(values, "col", [(j, j ^ k) for j in range(size)])


def col_blocks(values):
    size, me = lax.axis_size("col"), lax.axis_index("col")
    rows = values.shape[0] // size
    blocks = [lax.dynamic_slice_in_dim(values, (me ^ k) * rows, rows, 0) for k in range(size)]
    return [blocks[0]] + [swap(blocks[k], k) for k in range(1, size)]


def col_stack(parts):
    me = lax.axis_index("col")
    out = jnp.zeros((len(parts),) + parts[0].shape, parts[0].dtype)
    for k, part in enumerate(parts):
        out = lax.dynamic_update_slice_in_dim(out, part[None], me ^ k, 0)
    return out


def side_by_side(stacked):
    count, rows, cols = stacked.shape
    return jnp.transpose(stacked, (1, 0, 2)).reshape(rows, count * cols)


def col_gather(own):
    third = swap(own, 2)
    return [own, swap(own, 1), third, swap(third, 1)]


def col_total(part):
    far = swap(part(3).astype(BF), 1)
    near = swap(part(1).astype(BF), 1)
    passed = swap((part(2) + far.astype(F32)).astype(BF), 2)
    return part(0) + near.astype(F32) + passed.astype(F32)


def shift(values, d):
    size = lax.axis_size("row")
    return lax.ppermute(values, "row", [(i, (i + d) % size) for i in range(size)])


def row_gather(own):
    return [own] + [shift(own, d) for d in range(1, lax.axis_size("row"))]


def row_scatter(partial_sum):
    size = lax.axis_size("row")
    cols = partial_sum.shape[1] // size
    total = partial_sum[:, :cols]
    for d in range(1, size):
        total = total + shift(partial_sum[:, d * cols : (d + 1) * cols].astype(BF), -d).astype(F32)
    return total


def row_spread(matrix, axis):
    size, me = lax.axis_size("row"), lax.axis_index("row")
    count = matrix.shape[axis] // size
    parts = [
        lax.dynamic_slice_in_dim(matrix, ((me + d) % size) * count, count, axis) for d in range(size)
    ]
    return [parts[0]] + [shift(parts[d], d) for d in range(1, size)]


def row_return(matrix, axis):
    size, me = lax.axis_size("row"), lax.axis_index("row")
    count = matrix.shape[axis] // size
    blocks = [lax.slice_in_dim(matrix, d * count, (d + 1) * count, axis=axis) for d in range(size)]
    out = jnp.zeros((size,) + blocks[0].shape, matrix.dtype)
    for d in range(size):
        block = blocks[0] if d == 0 else shift(blocks[d], -d)
        out = lax.dynamic_update_slice_in_dim(out, block[None], (me + d) % size, 0)
    return out


def dp_total(values):
    size = lax.axis_size("dp")
    if size == 2:
        return values.astype(F32) + lax.ppermute(values, "dp", [(0, 1), (1, 0)]).astype(F32)
    return lax.psum(values.astype(F32), "dp")


def small_total(values):
    values = values + swap(values, 1)
    values = values + swap(values, 2)
    return dp_total(values)


def normalize(values):
    size = lax.axis_size("row")
    width = values.shape[1]
    own_mean = jnp.mean(values, axis=1)
    own_square = jnp.sum(jnp.square(values - own_mean[:, None]), axis=1)
    shared = row_gather(jnp.stack([own_mean, own_square]))
    center = sum(item[0] for item in shared) / size
    spread = sum(item[1] + width * jnp.square(item[0] - center) for item in shared) / (width * size)
    scale_row = lax.rsqrt(spread + epsilon)
    return (values - center[:, None]) * scale_row[:, None], scale_row


def normalize_back(grad_normed, normed, scale_row, gain_values):
    size = lax.axis_size("row")
    full_width = normed.shape[1] * size
    weighted = grad_normed * gain_values
    own = jnp.stack([jnp.sum(weighted, axis=1), jnp.sum(weighted * normed, axis=1)])
    totals = sum(row_gather(own)) / full_width
    return scale_row[:, None] * (weighted - totals[0][:, None] - normed * totals[1][:, None])


def gelu_slope(values):
    return 0.5 * (1.0 + lax.erf(values * root_half)) + values * inverse_root_tau * jnp.exp(
        -0.5 * values * values
    )


def block_mask(segment, positions, offset, block_len):
    own_segment = lax.dynamic_slice_in_dim(segment, offset, block_len, 0)
    own_position = offset + jnp.arange(block_len, dtype=jnp.int32)
    return (own_segment[:, None] == segment[None, :]) & (
        own_position[:, None] >= positions[None, :]
    )


def attend_forward(queries, key_rows, value_rows, segment, scaling):
    length = queries.shape[0]
    block_len = min(512, length)
    positions = jnp.arange(length, dtype=jnp.int32)

    def one_block(block_index):
        offset = block_index * block_len
        query_blk = lax.dynamic_slice_in_dim(queries, offset, block_len, 0)
        allowed = block_mask(segment, positions, offset, block_len)
        scores = contract(query_blk, key_rows, 1, 1) * scaling
        masked = jnp.where(allowed, scores, negative_fill)
        top_score = jnp.max(masked, axis=1, keepdims=True)
        exponent_terms = jnp.exp(masked - top_score)
        totals = jnp.sum(exponent_terms, axis=1, keepdims=True)
        softmax_rows = exponent_terms / totals
        attended = jnp.dot(softmax_rows.astype(BF), value_rows, preferred_element_type=F32)
        return (attended.astype(BF), (top_score + jnp.log(totals))[:, 0])

    attended, log_totals = lax.map(one_block, jnp.arange(length // block_len, dtype=jnp.int32))
    return (attended.reshape(length, queries.shape[1]), log_totals.reshape(length))


def attend_backward(queries, key_rows, value_rows, segment, log_totals, grad_heads, scaling):
    length, head_width = queries.shape
    block_len = min(512, length)
    positions = jnp.arange(length, dtype=jnp.int32)

    def one_block(carry, block_index):
        key_grad, value_grad = carry
        offset = block_index * block_len
        query_blk = lax.dynamic_slice_in_dim(queries, offset, block_len, 0)
        grad_blk = lax.dynamic_slice_in_dim(grad_heads, offset, block_len, 0)
        log_blk = lax.dynamic_slice_in_dim(log_totals, offset, block_len, 0)
        allowed = block_mask(segment, positions, offset, block_len)
        scores = contract(query_blk, key_rows, 1, 1) * scaling
        softmax_rows = jnp.where(allowed, jnp.exp(scores - log_blk[:, None]), 0.0)
        prob_grad = contract(grad_blk, value_rows, 1, 1)
        centered = jnp.sum(softmax_rows * prob_grad, axis=1, keepdims=True)
        score_grad = (softmax_rows * (prob_grad - centered)).astype(BF)
        query_grad = jnp.dot(score_grad, key_rows, preferred_element_type=F32) * scaling
        key_grad = key_grad + contract(score_grad, query_blk, 0, 0) * scaling
        value_grad = value_grad + contract(softmax_rows.astype(BF), grad_blk, 0, 0)
        return ((key_grad, value_grad), query_grad)

    zero_rows = jnp.zeros((length, head_width), F32)
    (key_grad, value_grad), query_grad = lax.scan(
        one_block, (zero_rows, zero_rows), jnp.arange(length // block_len, dtype=jnp.int32)
    )
    return (query_grad.reshape(length, head_width), key_grad, value_grad)


def local(
    inputs,
    segment_ids,
    attn_gain,
    attn_shift,
    query_weight,
    query_bias,
    key_weight,
    value_weight,
    value_bias,
    output_weight,
    output_bias,
    mlp_gain,
    mlp_shift,
    up_weight,
    up_bias,
    down_weight,
    down_bias,
    cotangent,
):
    assert lax.axis_size("col") == 4
    rows, cols = lax.axis_size("row"), lax.axis_size("col")
    zi, ci = lax.axis_index("row"), lax.axis_index("col")
    scaling = 1.0 / math.sqrt(HD)
    segment = segment_ids[0]
    length, share = inputs.shape
    tokens = length // cols
    width = share * cols
    hid = up_weight.shape[1] // rows

    vectors = jnp.stack(
        [attn_gain, attn_shift, mlp_gain, mlp_shift, output_bias, down_bias]
        + [jnp.zeros_like(attn_gain)] * 10
    )
    parts = []
    for k in range(cols):
        begin = (ci ^ k) * tokens
        part = jnp.concatenate(
            [
                lax.dynamic_slice_in_dim(inputs, begin, tokens, 0),
                lax.dynamic_slice_in_dim(cotangent, begin, tokens, 0),
                vectors,
            ]
        )
        parts.append(part if k == 0 else swap(part, k))
    arrived = side_by_side(col_stack(parts)).astype(F32)
    resid, grad_out = arrived[:tokens], arrived[tokens : 2 * tokens]
    vectors = arrived[2 * tokens :]
    attn_gain_f, attn_shift_f, mlp_gain_f, mlp_shift_f, output_bias_f, down_bias_f = (
        vectors[i] for i in range(6)
    )

    def with_rows(parts, axis):
        return jnp.concatenate(parts, axis=axis)

    heads = [lax.dynamic_slice_in_dim(b, zi * HD, HD, 0) for b in (query_bias, value_bias)]
    units = lax.dynamic_slice_in_dim(up_bias, zi * hid, hid, 0)
    own_bias = jnp.concatenate(heads + [units])
    biases = [own_bias] + [swap(own_bias, k) for k in range(1, cols)]
    qkv_local = jnp.concatenate(
        [m.reshape(width, rows, HD) for m in (query_weight, key_weight, value_weight)], axis=2
    ).reshape(width, rows * 3 * HD)
    qkv_parts = col_gather(with_rows(row_spread(qkv_local, 1), 0))
    qkv_w = with_rows(qkv_parts, 1)
    out_w = with_rows(col_gather(with_rows(row_spread(output_weight, 0), 1)), 0)

    attn_hat, attn_scale = normalize(resid)
    h1 = with_rows(row_gather((attn_hat * attn_gain_f + attn_shift_f).astype(BF)), 1)
    up_local, down_local = after((up_weight, down_weight), h1)
    up_w = with_rows(col_gather(with_rows(row_spread(up_local, 1), 0)), 1)
    down_own = with_rows(row_spread(down_local, 0), 1)
    down_w = with_rows(col_gather(down_own), 0)
    grad_rows = with_rows(row_gather(after(grad_out.astype(BF), down_own)), 1)

    head_bias = [
        jnp.concatenate([b[:HD], jnp.zeros_like(b[:HD]), b[HD : 2 * HD]]).astype(F32) for b in biases
    ]
    projected = contract(h1, qkv_w, 1, 0) + jnp.concatenate(head_bias)
    projected = projected.astype(BF)
    head_parts = [
        p if k == 0 else swap(p, k) for k, p in enumerate(jnp.split(projected, cols, axis=1))
    ]
    head_rows = col_stack(head_parts).reshape(length, 3 * HD)
    queries, key_rows, value_rows = jnp.split(head_rows, 3, axis=1)
    attended, log_totals = attend_forward(queries, key_rows, value_rows, segment, scaling)
    attended_all = with_rows(col_blocks(attended), 1)
    after_attn = resid + row_scatter(contract(attended_all, out_w, 1, 0)) + output_bias_f

    mlp_hat, mlp_scale = normalize(after_attn)
    h2 = with_rows(row_gather((mlp_hat * mlp_gain_f + mlp_shift_f).astype(BF)), 1)
    unit_bias = jnp.concatenate([b[2 * HD :] for b in biases]).astype(F32)
    pre_act = contract(h2, up_w, 1, 0) + unit_bias
    hidden = jax.nn.gelu(pre_act, approximate=False).astype(BF)
    unit_grad = contract(grad_rows, down_w, 1, 1)
    pre_grad = (unit_grad * gelu_slope(pre_act)).astype(BF)
    h2_grad = row_scatter(contract(pre_grad, up_w, 1, 1))
    mlp_back = normalize_back(h2_grad, mlp_hat, mlp_scale, mlp_gain_f)
    after_grad = grad_out + mlp_back
    after_rows = with_rows(row_gather(after_grad.astype(BF)), 1)

    result = after_attn + row_scatter(contract(hidden, down_w, 1, 0)) + down_bias_f

    def columns(matrix, k, count):
        return matrix[:, k * count : (k + 1) * count]

    down_grad = dp_total(
        row_return(
            col_total(lambda k: contract(columns(hidden, k, hid), grad_rows, 0, 0)).astype(BF), 1
        )
    ).reshape(rows * hid, width)
    up_grad = side_by_side(
        dp_total(
            row_return(col_total(lambda k: contract(h2, columns(pre_grad, k, hid), 0, 0)).astype(BF), 0)
        )
    )

    head_grad = contract(after_rows, out_w, 1, 1).astype(BF)
    head_grad = col_stack(
        [g if k == 0 else swap(g, k) for k, g in enumerate(jnp.split(head_grad, cols, axis=1))]
    ).reshape(length, HD)
    output_grad = dp_total(
        row_return(
            col_total(lambda k: contract(columns(attended_all, k, HD), after_rows, 0, 0)).astype(BF), 1
        )
    ).reshape(rows * HD, width)
    query_grad, key_grad, value_grad = attend_backward(
        queries, key_rows, value_rows, segment, log_totals, head_grad, scaling
    )
    packed = jnp.concatenate([query_grad, key_grad, value_grad], axis=1).astype(BF)
    packed_rows = with_rows(col_blocks(packed), 1)
    h1_grad = row_scatter(contract(packed_rows, qkv_w, 1, 1))
    attn_back = normalize_back(h1_grad, attn_hat, attn_scale, attn_gain_f)
    input_grad = after_grad + attn_back
    qkv_grad = dp_total(
        row_return(
            col_total(lambda k: contract(h1, columns(packed_rows, k, 3 * HD), 0, 0)).astype(BF), 0
        )
    )
    query_grad_w, key_grad_w, value_grad_w = (
        side_by_side(qkv_grad[:, :, i * HD : (i + 1) * HD]) for i in range(3)
    )

    def to_columns(values):
        blocks = jnp.transpose(values.reshape(tokens, cols, share), (1, 0, 2))
        blocks = blocks.reshape(cols * tokens, share)
        return col_stack(col_blocks(blocks)).reshape(length, share)

    result_out = to_columns(result.astype(BF))
    input_grad_out = to_columns(input_grad.astype(BF)).astype(F32)

    packed_sums = jnp.sum(packed.astype(F32), axis=0)
    head_sums = jnp.concatenate([packed_sums[:HD], packed_sums[2 * HD :]])
    vector_sums = jnp.stack(
        [
            jnp.sum(h1_grad * attn_hat, axis=0),
            jnp.sum(h1_grad, axis=0),
            jnp.sum(after_grad, axis=0),
            jnp.sum(h2_grad * mlp_hat, axis=0),
            jnp.sum(h2_grad, axis=0),
            jnp.sum(grad_out, axis=0),
        ]
    )
    own_head = lax.dynamic_update_slice(jnp.zeros((cols, 2 * HD), F32), head_sums[None], (ci, 0))
    unit_sums = col_stack(jnp.split(jnp.sum(pre_grad.astype(F32), axis=0), cols))
    totals = small_total(
        jnp.concatenate([vector_sums.reshape(-1), own_head.reshape(-1), unit_sums.reshape(-1)])
    )
    cut = 6 * width
    vector_totals = lax.dynamic_slice_in_dim(totals[:cut].reshape(6, width), ci * share, share, 1)
    head_totals = totals[cut : cut + cols * 2 * HD].reshape(cols, 2 * HD)
    unit_totals = totals[cut + cols * 2 * HD :].reshape(cols, hid)
    shared = lax.dynamic_slice_in_dim(
        jnp.concatenate([head_totals, unit_totals], axis=1), ci, 1, 0
    )[0]
    shared_rows = jnp.zeros((rows, shared.shape[0]), F32)
    for d, item in enumerate(row_gather(shared)):
        shared_rows = lax.dynamic_update_slice(shared_rows, item[None], ((zi - d) % rows, 0))
    return (
        result_out,
        input_grad_out,
        vector_totals[0],
        vector_totals[1],
        query_grad_w,
        shared_rows[:, :HD].reshape(-1),
        key_grad_w,
        value_grad_w,
        shared_rows[:, HD : 2 * HD].reshape(-1),
        output_grad,
        vector_totals[2],
        vector_totals[3],
        vector_totals[4],
        up_grad,
        shared_rows[:, 2 * HD :].reshape(-1),
        down_grad,
        vector_totals[5],
    )


def solution(mesh):
    wide, tall = P("row", "col"), P("col", "row")
    both, tokens = P(("row", "col")), P("dp", ("row", "col"))
    return jax.shard_map(
        local,
        mesh=mesh,
        in_specs=(
            tokens,
            P("dp", None),
            both,
            both,
            wide,
            P("col"),
            wide,
            wide,
            P("col"),
            tall,
            both,
            both,
            both,
            wide,
            P("col"),
            tall,
            both,
            tokens,
        ),
        out_specs=(
            tokens,
            tokens,
            both,
            both,
            wide,
            P("col"),
            wide,
            wide,
            P("col"),
            tall,
            both,
            both,
            both,
            wide,
            P("col"),
            tall,
            both,
        ),
        check_vma=False,
    )
```
